256 devices in a mesh: loop: 16 (over y, x), dp: 16 (over z, core).
Axes of the slice: x: 4, y: 4, z: 8, core: 2. Of those that a mesh axis runs over, the one named last changes fastest.
Arguments:
- tokens: bfloat16 [3584, 8192], P('dp', 'loop'), may hold values from -8 to 8
- weight: bfloat16 [8192, 14336], P('loop', 'dp'), as said below
- rounding: float32 [8192, 14336], P('loop', 'dp'), may hold values from -6 to 6
- floor_codes: int32 [8192, 14336], P('loop', 'dp'), may hold values from -1 to 15
- scale_codes: int32 [14336], P('dp'), may hold values from 12 to 15
- zero_codes: int32 [14336], P('dp'), may hold values from 0 to 15
- block_mask: int32 [128, 224], P('loop', 'dp'), may hold values from 0 to 1, as said below
Outputs:
- refined: float32 [8192, 14336], P('loop', 'dp')
The draws below stay inside these ranges and needn't reach their ends.
Inputs may be any that keep to these rules, and one draw needn't show every extreme that they name: weight equals scales times (floor_codes - zero_point + a fraction in [0, 1)), then is rounded to bfloat16. `block_mask`: the share of surviving blocks differs between column blocks.
All inputs are finite; a program needn't handle non-finite values.
Results may differ from the reference program's by a relative error of at most 0.019.
Values may be sent and summed in bfloat16 or wider, within the bound.
A program may use at most 128 MiB of HBM per device.

```python
import jax
import jax.numpy as jnp
from jax import lax

D = 8192
FF = 14336
BLOCK = 64
ITERS = 2
TOKENS = 3584
N_LOOP = 16


def grid_codes(key):
    floor_codes = jax.random.randint(jax.random.fold_in(key, 11), (D, FF), -1, 16, dtype=jnp.int32)
    scale_codes = jax.random.randint(jax.random.fold_in(key, 12), (FF,), 12, 16, dtype=jnp.int32)
    zero_codes = jax.random.randint(jax.random.fold_in(key, 13), (FF,), 0, 16, dtype=jnp.int32)
    return (floor_codes, scale_codes, zero_codes)


def draw_floor_codes(key, part):
    return grid_codes(key)[0]


def draw_scale_codes(key, part):
    return grid_codes(key)[1]


def draw_zero_codes(key, part):
    return grid_codes(key)[2]


def draw_weight(key, part):
    floor_codes, scale_codes, zero_codes = grid_codes(key)
    scales = 0.02 * jnp.exp2(scale_codes.astype(jnp.float32) * 0.25)
    fraction = jax.random.uniform(jax.random.fold_in(key, 14), (D, FF), jnp.float32, 0.0, 1.0)
    values = scales[None, :] * (floor_codes.astype(jnp.float32) - zero_codes.astype(jnp.float32)[None, :] + fraction)
    return values.astype(jnp.bfloat16)


def draw_block_mask(key, part):
    density = jax.random.randint(jax.random.fold_in(key, 21), (FF // BLOCK,), 1, 8, dtype=jnp.int32)
    rolled = jax.random.randint(jax.random.fold_in(key, 22), (D // BLOCK, FF // BLOCK), 0, 8, dtype=jnp.int32)
    return (rolled < density[None, :]).astype(jnp.int32)


def block_scale(key, extent, split, least, high):
    def one(position, shards_of):
        heights = jax.random.uniform(jax.random.fold_in(jax.random.fold_in(key, 6), position), (shards_of,), jnp.float32, least / len(split), high / len(split))
        return jnp.repeat(jnp.exp(heights), extent[position] // shards_of).reshape((-1,) + (1,) * (len(extent) - position - 1))

    loudness = one(*split[0])
    for cut in split[1:]:
        loudness = loudness * one(*cut)
    return loudness


def centred(key, extent, deviation, limit, pieces=(), held_as=jnp.bfloat16):
    level = block_scale(key, extent, pieces, -0.22, 0.18) if pieces else 1.0
    entries = jax.random.normal(key, extent, jnp.float32) * deviation * level
    return jnp.minimum(jnp.maximum(entries, -limit), limit).astype(held_as)


def setup_inputs(seed: int = 0) -> dict:
    streams_of = jax.random.split(jax.random.key(seed), 8)
    tokens = centred(streams_of[0], (TOKENS, D), 2.0, 8.0, ((0, 16), (1, 16)))
    weight = draw_weight(jax.random.fold_in(streams_of[7], 71), 0)
    rounding = centred(streams_of[2], (D, FF), 1.0, 6.0, ((0, 16), (1, 16)), jnp.float32)
    floor_codes = draw_floor_codes(jax.random.fold_in(streams_of[7], 71), 0)
    scale_codes = draw_scale_codes(jax.random.fold_in(streams_of[7], 71), 0)
    zero_codes = draw_zero_codes(jax.random.fold_in(streams_of[7], 71), 0)
    block_mask = draw_block_mask(jax.random.fold_in(streams_of[7], 71), 0)
    return {"tokens": tokens, "weight": weight, "rounding": rounding, "floor_codes": floor_codes, "scale_codes": scale_codes, "zero_codes": zero_codes, "block_mask": block_mask}


step_rate = 20.0
reg_weight = 0.05
base_scale = 0.02


def expand(block_mask):
    row_blocks, col_blocks = block_mask.shape
    spread = jnp.broadcast_to(block_mask[:, None, :, None], (row_blocks, BLOCK, col_blocks, BLOCK))
    return spread.reshape(row_blocks * BLOCK, col_blocks * BLOCK).astype(jnp.float32)


def refine(tokens, weight, rounding, floor_codes, scales, zero_point, kept_mask):
    panel_width = weight.shape[1]
    floors = floor_codes.astype(jnp.float32)
    in_range = ((floor_codes >= 0) & (floor_codes <= 14)).astype(jnp.float32)
    target = weight.astype(jnp.float32)
    grouped = tokens.astype(jnp.float32).reshape(TOKENS, N_LOOP, D // N_LOOP)
    for iteration in range(ITERS):
        relaxed = jax.nn.sigmoid(rounding)
        levels = jnp.clip(floors + relaxed, 0.0, 15.0)
        w_delta = (kept_mask * (scales[None, :] * (levels - zero_point[None, :]) - target)).astype(jnp.bfloat16)
        delta_groups = w_delta.astype(jnp.float32).reshape(N_LOOP, D // N_LOOP, panel_width)
        partials = jnp.einsum("tkd,kdc->ktc", grouped, delta_groups, precision=lax.Precision.HIGHEST)
        rounded = lax.optimization_barrier(partials.astype(jnp.bfloat16))
        residual = jnp.sum(rounded.astype(jnp.float32), axis=0)
        scaled_err = ((2.0 / TOKENS) * residual).astype(jnp.bfloat16)
        gradient = jnp.dot(tokens.T, scaled_err, preferred_element_type=jnp.float32)
        centered = 2.0 * relaxed - 1.0
        descent = gradient * scales[None, :] * in_range - reg_weight * 8.0 * centered ** 3
        rounding = rounding - step_rate * kept_mask * descent * relaxed * (1.0 - relaxed)
    return rounding


def reference(tokens, weight, rounding, floor_codes, scale_codes, zero_codes, block_mask):
    panel_width = FF // 8
    scales_all = base_scale * jnp.exp2(scale_codes.astype(jnp.float32) * 0.25)
    zero_all = zero_codes.astype(jnp.float32)

    def one_panel(panel_index):
        first_col = (panel_index * panel_width).astype(jnp.int32)
        first_block = (panel_index * (panel_width // BLOCK)).astype(jnp.int32)
        weight_panel = lax.dynamic_slice_in_dim(weight, first_col, panel_width, 1)
        rounding_panel = lax.dynamic_slice_in_dim(rounding, first_col, panel_width, 1)
        floor_panel = lax.dynamic_slice_in_dim(floor_codes, first_col, panel_width, 1)
        scale_panel = lax.dynamic_slice_in_dim(scales_all, first_col, panel_width, 0)
        zero_panel = lax.dynamic_slice_in_dim(zero_all, first_col, panel_width, 0)
        mask_panel = lax.dynamic_slice_in_dim(block_mask, first_block, panel_width // BLOCK, 1)
        return refine(tokens, weight_panel, rounding_panel, floor_panel, scale_panel, zero_panel, expand(mask_panel))

    panels = lax.map(one_panel, jnp.arange(8, dtype=jnp.int32))
    return jnp.transpose(panels, (1, 0, 2)).reshape(D, FF)
```

```python
import jax
import jax.numpy as jnp
from jax import lax
from jax.experimental import pallas as pl
from jax.experimental.pallas import tpu as pltpu
from jax.sharding import PartitionSpec as P

MESH = pl.DeviceIdType.MESH
BLOCK = 64
ITERS = 2
RING = 4
DEPTH = 8

step_rate = 20.0
reg_weight = 0.05
base_scale = 0.02

ROWS = 512
COLS = 896
TOKENS = 3584
PIECE = 112
WAVE = 4 * PIECE
SPLIT = 64
HALF = ROWS // 2
TILE = 16


def kernel(
    tok, wt, v_in, fl, sc, zp, km, out,
    X, W, RS, RCA, RCB, RFP, RFM, E, Racc, Gacc, GS, GCA, GCB, GFP, GFM,
    x1_send, x1_recv, z_send, z_recv, w_send, w_recv, r_send, r_recv, e_send, e_recv, g_send, g_recv,
):
    loop = lax.axis_index("loop")
    dp = lax.axis_index("dp")
    y, x = loop // 4, lax.rem(loop, 4)
    z, c = dp // 2, lax.rem(dp, 2)
    g = x * (1 - c) + y * c
    r = y * (1 - c) + x * c

    def device(gp, rp):
        return (gp * (1 + 3 * c) + rp * (4 - 3 * c), dp)

    g_next = device(lax.rem(g + 1, 4), r)
    g_prev = device(lax.rem(g + 3, 4), r)
    r_next = device(g, lax.rem(r + 1, 4))
    r_prev = device(g, lax.rem(r + 3, 4))
    z_next = (loop, lax.rem(z + 1, DEPTH) * 2 + c)
    z_prev = (loop, lax.rem(z + DEPTH - 1, DEPTH) * 2 + c)

    pending = []

    def send(src, dst, send_sem, recv_sem, to):
        copy = pltpu.make_async_remote_copy(
            src_ref=src, dst_ref=dst, send_sem=send_sem, recv_sem=recv_sem, device_id=to, device_id_type=MESH
        )
        copy.start()
        pending.append(copy)
        return copy

    def arrived(ref, sem):
        pltpu.make_async_copy(ref, ref, sem).wait()

    exchange = []
    for j in range(2):
        goal = 2 * c + j
        for role in range(2):
            if role == 0:
                to = (y * 4 + goal, z * 2)
                slot = lax.rem(x - goal + 4, 4)
                mine = (goal - x) * (goal - x) + c
            else:
                to = (goal * 4 + x, z * 2 + 1)
                slot = lax.rem(y - goal + 4, 4)
                mine = (goal - y) * (goal - y) + (1 - c)
            src = tok.at[pl.ds(j * PIECE, PIECE), :]
            dst = X.at[slot, pl.ds(0, PIECE), :]
            sem = x1_recv.at[slot]
            remote = pltpu.make_async_remote_copy(
                src_ref=src, dst_ref=dst, send_sem=x1_send.at[2 * j + role], recv_sem=sem,
                device_id=to, device_id_type=MESH,
            )
            local = pltpu.make_async_copy(src, dst, sem)
            exchange.append((mine, remote))

            @pl.when(mine == 0)
            def _():
                local.start()

            @pl.when(mine != 0)
            def _():
                remote.start()

    def piece(slot, half):
        return X.at[pl.ds(2 * half, 2), pl.ds(slot * PIECE, PIECE), :]

    def z_forward(sign, slot, half):
        to = z_next if sign > 0 else z_prev
        if sign > 0:
            there = {0: 1, 1: 3, 3: 5, 5: 7}[slot]
        else:
            there = {0: 2, 2: 4, 4: 6, 6: 7}[slot]
        index = 2 * there + half
        return send(piece(slot, half), piece(there, half), z_send.at[index], z_recv.at[index], to)

    def z_wait(slot, half):
        arrived(piece(slot, half), z_recv.at[2 * slot + half])

    scale = sc[...]
    zero = zp[...]

    def delta(tile, v):
        rows = pl.ds(pl.multiple_of(tile * TILE, TILE), TILE)
        kept = km[pl.ds(tile // (BLOCK // TILE), 1), :]
        relaxed = jax.nn.sigmoid(v)
        levels = jnp.clip(fl[rows, :].astype(jnp.float32) + relaxed, 0.0, 15.0)
        return (kept * (scale * (levels - zero) - wt[rows, :].astype(jnp.float32))).astype(jnp.bfloat16)

    def first_delta():
        def body(tile, carry):
            rows = pl.ds(pl.multiple_of(tile * TILE, TILE), TILE)
            W[0, 0, rows, :] = delta(tile, v_in[rows, :])
            return carry

        lax.fori_loop(0, ROWS // TILE, body, 0)

    def update(it):
        old = v_in if it == 0 else out

        def body(tile, carry):
            rows = pl.ds(pl.multiple_of(tile * TILE, TILE), TILE)
            v = old[rows, :]
            gradient = (
                Gacc[0, rows, :] + GFP[it, rows, :].astype(jnp.float32) + GFM[it, rows, :].astype(jnp.float32)
            )
            relaxed = jax.nn.sigmoid(v)
            codes = fl[rows, :]
            in_range = ((codes >= 0) & (codes <= 14)).astype(jnp.float32)
            kept = km[pl.ds(tile // (BLOCK // TILE), 1), :]
            centered = 2.0 * relaxed - 1.0
            descent = gradient * scale * in_range - reg_weight * 8.0 * (centered * centered * centered)
            v = v - step_rate * kept * descent * relaxed * (1.0 - relaxed)
            out[rows, :] = v
            if it + 1 < ITERS:
                W[it + 1, 0, rows, :] = delta(tile, v)
            return carry

        lax.fori_loop(0, ROWS // TILE, body, 0)

    TOP, LOW = pl.ds(0, HALF), pl.ds(HALF, HALF)

    def w_copy(it, here, there, rows, index, to):
        return send(W.at[it, here, rows, :], W.at[it, there, rows, :], w_send.at[it, index], w_recv.at[it, index], to)

    def w_start(it):
        w_copy(it, 0, 3, TOP, 0, g_next)
        w_copy(it, 0, 1, LOW, 1, g_prev)
        w_copy(it, 0, 3, LOW, 2, g_next)
        w_copy(it, 0, 1, TOP, 3, g_prev)

    def w_relay(it):
        arrived(W.at[it, 3, TOP, :], w_recv.at[it, 0])
        w_copy(it, 3, 2, TOP, 4, g_next)
        arrived(W.at[it, 1, LOW, :], w_recv.at[it, 1])
        w_copy(it, 1, 2, LOW, 5, g_prev)

    def w_near(it):
        arrived(W.at[it, 3, LOW, :], w_recv.at[it, 2])
        arrived(W.at[it, 1, TOP, :], w_recv.at[it, 3])

    def w_far(it):
        arrived(W.at[it, 2, TOP, :], w_recv.at[it, 4])
        arrived(W.at[it, 2, LOW, :], w_recv.at[it, 5])

    def residual(it, wave, slots, first):
        rows = pl.ds(wave * WAVE, WAVE)
        total = None
        for slot in slots:
            part = jnp.dot(X[slot, rows, :], W[it, slot], preferred_element_type=jnp.float32)
            total = part if total is None else total + part
        Racc[rows, :] = total if first else Racc[rows, :] + total

    def chunk(wave, d):
        return pl.multiple_of(wave * WAVE + lax.rem(r + d, 4) * PIECE, 16)

    A, B = pl.ds(0, SPLIT), pl.ds(SPLIT, PIECE - SPLIT)

    def r_copy(it, wave, d, half, dst, index, to):
        return send(RS.at[it, wave, d - 1, half, :], dst, r_send.at[it, wave, index], r_recv.at[it, wave, index], to)

    def r_start(it, wave):
        RS[it, wave, 1] = Racc[pl.ds(chunk(wave, 2), PIECE), :].astype(jnp.bfloat16)
        r_copy(it, wave, 2, A, RCA.at[it, wave], 0, r_next)
        r_copy(it, wave, 2, B, RCB.at[it, wave], 1, r_prev)
        RS[it, wave, 0, B, :] = Racc[pl.ds(pl.multiple_of(chunk(wave, 1) + SPLIT, 16), PIECE - SPLIT), :].astype(jnp.bfloat16)
        r_copy(it, wave, 1, B, RFP.at[it, wave, B, :], 2, r_next)
        RS[it, wave, 2, A, :] = Racc[pl.ds(chunk(wave, 3), SPLIT), :].astype(jnp.bfloat16)
        r_copy(it, wave, 3, A, RFM.at[it, wave, A, :], 3, r_prev)

    def r_middle(it, wave):
        arrived(RCA.at[it, wave], r_recv.at[it, wave, 0])
        RS[it, wave, 0, A, :] = (
            Racc[pl.ds(chunk(wave, 1), SPLIT), :] + RCA[it, wave].astype(jnp.float32)
        ).astype(jnp.bfloat16)
        r_copy(it, wave, 1, A, RFP.at[it, wave, A, :], 4, r_next)
        arrived(RCB.at[it, wave], r_recv.at[it, wave, 1])
        RS[it, wave, 2, B, :] = (
            Racc[pl.ds(pl.multiple_of(chunk(wave, 3) + SPLIT, 16), PIECE - SPLIT), :]
            + RCB[it, wave].astype(jnp.float32)
        ).astype(jnp.bfloat16)
        r_copy(it, wave, 3, B, RFM.at[it, wave, B, :], 5, r_prev)

    def e_copy(it, wave, d, half, index, to):
        start = chunk(wave, d) + (0 if half == 0 else SPLIT)
        rows = pl.ds(pl.multiple_of(start, 16), SPLIT if half == 0 else PIECE - SPLIT)
        return send(E.at[it, rows, :], E.at[it, rows, :], e_send.at[it, wave, index], e_recv.at[it, wave, index], to)

    def e_wait(it, wave, d, half, index):
        start = chunk(wave, d) + (0 if half == 0 else SPLIT)
        rows = pl.ds(pl.multiple_of(start, 16), SPLIT if half == 0 else PIECE - SPLIT)
        arrived(E.at[it, rows, :], e_recv.at[it, wave, index])

    def r_finish(it, wave):
        arrived(RFP.at[it, wave, B, :], r_recv.at[it, wave, 2])
        arrived(RFM.at[it, wave, A, :], r_recv.at[it, wave, 3])
        arrived(RFP.at[it, wave, A, :], r_recv.at[it, wave, 4])
        arrived(RFM.at[it, wave, B, :], r_recv.at[it, wave, 5])
        rows = pl.ds(chunk(wave, 0), PIECE)
        total = Racc[rows, :] + RFP[it, wave].astype(jnp.float32) + RFM[it, wave].astype(jnp.float32)
        E[it, rows, :] = (2.0 / TOKENS * total).astype(jnp.bfloat16)
        e_copy(it, wave, 0, 0, 0, r_next)
        e_copy(it, wave, 0, 1, 1, r_prev)
        e_copy(it, wave, 0, 1, 2, r_next)
        e_copy(it, wave, 0, 0, 3, r_prev)

    def e_relay(it, wave):
        e_wait(it, wave, 3, 0, 0)
        e_copy(it, wave, 3, 0, 4, r_next)
        e_wait(it, wave, 1, 1, 1)
        e_copy(it, wave, 1, 1, 5, r_prev)

    def e_end(it, wave):
        e_wait(it, wave, 3, 1, 2)
        e_wait(it, wave, 1, 0, 3)
        e_wait(it, wave, 2, 0, 4)
        e_wait(it, wave, 2, 1, 5)

    def gradient(it, wave, slot):
        rows = pl.ds(wave * WAVE, WAVE)
        part = lax.dot_general(
            X[slot, rows, :], E[it, rows, :], (((0,), (0,)), ((), ())), preferred_element_type=jnp.float32
        )
        Gacc[slot] = part if wave == 0 else Gacc[slot] + part

    def g_copy(it, d, half, dst, index, to):
        return send(GS.at[it, d - 1, half, :], dst, g_send.at[it, index], g_recv.at[it, index], to)

    def g_reduce(it):
        gradient(it, 1, 2)
        GS[it, 1] = Gacc[2].astype(jnp.bfloat16)
        g_copy(it, 2, TOP, GCA.at[it], 0, g_next)
        g_copy(it, 2, LOW, GCB.at[it], 1, g_prev)
        gradient(it, 1, 1)
        GS[it, 0, LOW, :] = Gacc[1, LOW, :].astype(jnp.bfloat16)
        g_copy(it, 1, LOW, GFP.at[it, LOW, :], 2, g_next)
        gradient(it, 1, 3)
        GS[it, 2, TOP, :] = Gacc[3, TOP, :].astype(jnp.bfloat16)
        g_copy(it, 3, TOP, GFM.at[it, TOP, :], 3, g_prev)
        arrived(GCA.at[it], g_recv.at[it, 0])
        GS[it, 0, TOP, :] = (Gacc[1, TOP, :] + GCA[it].astype(jnp.float32)).astype(jnp.bfloat16)
        g_copy(it, 1, TOP, GFP.at[it, TOP, :], 4, g_next)
        arrived(GCB.at[it], g_recv.at[it, 1])
        GS[it, 2, LOW, :] = (Gacc[3, LOW, :] + GCB[it].astype(jnp.float32)).astype(jnp.bfloat16)
        g_copy(it, 3, LOW, GFM.at[it, LOW, :], 5, g_prev)
        gradient(it, 1, 0)
        arrived(GFP.at[it, LOW, :], g_recv.at[it, 2])
        arrived(GFM.at[it, TOP, :], g_recv.at[it, 3])
        arrived(GFP.at[it, TOP, :], g_recv.at[it, 4])
        arrived(GFM.at[it, LOW, :], g_recv.at[it, 5])

    first_delta()
    w_start(0)
    for slot in range(RING):
        arrived(X.at[slot, pl.ds(0, PIECE), :], x1_recv.at[slot])
    for half in range(2):
        z_forward(1, 0, half)
        z_forward(-1, 0, 1 - half)
    w_relay(0)
    for half in range(2):
        z_wait(1, half)
        z_forward(1, 1, half)
        z_wait(2, 1 - half)
        z_forward(-1, 2, 1 - half)
    w_near(0)
    w_far(0)
    for half in range(2):
        z_wait(3, half)
        z_forward(1, 3, half)
        z_wait(4, 1 - half)
        z_forward(-1, 4, 1 - half)
    residual(0, 0, (0, 1, 2, 3), True)
    r_start(0, 0)
    r_middle(0, 0)
    r_finish(0, 0)
    z_wait(5, 0)
    z_forward(1, 5, 0)
    z_wait(6, 1)
    z_forward(-1, 6, 1)
    e_relay(0, 0)
    e_end(0, 0)
    for slot in range(RING):
        gradient(0, 0, slot)
    z_wait(5, 1)
    z_wait(6, 0)
    z_wait(7, 0)
    z_wait(7, 1)
    residual(0, 1, (0, 1, 2, 3), True)
    r_start(0, 1)
    r_middle(0, 1)
    r_finish(0, 1)
    e_relay(0, 1)
    e_end(0, 1)
    g_reduce(0)
    update(0)

    w_start(1)
    residual(1, 0, (0,), True)
    residual(1, 1, (0,), True)
    w_relay(1)
    w_near(1)
    residual(1, 0, (1, 3), False)
    residual(1, 1, (1, 3), False)
    w_far(1)
    residual(1, 0, (2,), False)
    r_start(1, 0)
    residual(1, 1, (2,), False)
    r_start(1, 1)
    r_middle(1, 0)
    r_middle(1, 1)
    r_finish(1, 0)
    r_finish(1, 1)
    e_relay(1, 0)
    e_relay(1, 1)
    e_end(1, 0)
    for slot in range(RING):
        gradient(1, 0, slot)
    e_end(1, 1)
    g_reduce(1)
    update(1)

    for copy in pending:
        copy.wait_send()
    for mine, remote in exchange:

        @pl.when(mine != 0)
        def _():
            remote.wait_send()


def per_device(tokens, weight, rounding, floor_codes, scale_codes, zero_codes, block_mask):
    scales = base_scale * jnp.exp2(scale_codes.astype(jnp.float32) * 0.25)
    zero_point = zero_codes.astype(jnp.float32)
    kept = jnp.repeat(block_mask.astype(jnp.float32), BLOCK, axis=1)
    whole = pl.BlockSpec(memory_space=pltpu.VMEM)
    bf16, f32 = jnp.bfloat16, jnp.float32
    dma = pltpu.SemaphoreType.DMA
    return pl.pallas_call(
        kernel,
        out_shape=jax.ShapeDtypeStruct((ROWS, COLS), f32),
        in_specs=[whole] * 7,
        out_specs=whole,
        scratch_shapes=[
            pltpu.VMEM((RING, 2 * WAVE, ROWS), bf16),
            pltpu.VMEM((ITERS, RING, ROWS, COLS), bf16),
            pltpu.VMEM((ITERS, 2, 3, PIECE, COLS), bf16),
            pltpu.VMEM((ITERS, 2, SPLIT, COLS), bf16),
            pltpu.VMEM((ITERS, 2, PIECE - SPLIT, COLS), bf16),
            pltpu.VMEM((ITERS, 2, PIECE, COLS), bf16),
            pltpu.VMEM((ITERS, 2, PIECE, COLS), bf16),
            pltpu.VMEM((ITERS, 2 * WAVE, COLS), bf16),
            pltpu.VMEM((2 * WAVE, COLS), f32),
            pltpu.VMEM((RING, ROWS, COLS), f32),
            pltpu.VMEM((ITERS, 3, ROWS, COLS), bf16),
            pltpu.VMEM((ITERS, HALF, COLS), bf16),
            pltpu.VMEM((ITERS, HALF, COLS), bf16),
            pltpu.VMEM((ITERS, ROWS, COLS), bf16),
            pltpu.VMEM((ITERS, ROWS, COLS), bf16),
            dma((4,)), dma((4,)), dma((16,)), dma((16,)),
            dma((ITERS, 6)), dma((ITERS, 6)),
            dma((ITERS, 2, 6)), dma((ITERS, 2, 6)),
            dma((ITERS, 2, 6)), dma((ITERS, 2, 6)),
            dma((ITERS, 6)), dma((ITERS, 6)),
        ],
        compiler_params=pltpu.CompilerParams(has_side_effects=True, vmem_limit_bytes=67043328),
    )(tokens, weight, rounding, floor_codes, scales[None, :], zero_point[None, :], kept)


def solution(mesh):
    placed = (
        P("dp", "loop"),
        P("loop", "dp"),
        P("loop", "dp"),
        P("loop", "dp"),
        P("dp"),
        P("dp"),
        P("loop", "dp"),
    )
    return jax.shard_map(
        per_device, mesh=mesh, in_specs=placed, out_specs=P("loop", "dp"), check_vma=False
    )
```
